32 devices in a mesh: blk: 8 (over y, x, core), space: 4 (over z).
Axes of the slice: x: 2, y: 2, z: 4, core: 2. Of those that a mesh axis runs over, the one named last changes fastest.
Arguments:
- electrons: bfloat16 [8, 8, 2, 64, 4096], P('blk', None, None, 'space'), may hold values from -4 to 4
- holes: bfloat16 [8, 8, 2, 64, 4096], P('blk', None, None, 'space'), may hold values from -4 to 4
- pair_order: int32 [8, 2], P('blk'), may hold values from 0 to 1, each once within a row
Outputs:
- potential: float32 [8, 2, 64, 64, 128], P('blk', None, 'space')
- coulomb: float32 [8, 2, 2, 2], P('blk')
The draws below stay inside these ranges and needn't reach their ends.
Inputs may be any that keep to these rules, and one draw needn't show every extreme that they name: `pair_order`: each row lists every candidate once.
All inputs are finite; a program needn't handle non-finite values.
Results may differ from the reference program's by a relative error of at most 0.0003.
Values may be sent and summed in bfloat16 or wider, within the bound.
A program may use at most 64 MiB of HBM per device.

```python
import math
import jax
import jax.numpy as jnp
from jax import lax

BANDS = 8
NX = 64
NY = 64
NZ = 64
EG = 1
HG = 1
GROUPS = 8
E = 8
H = 8
P_SIZE = 2


def dot_envelopes(key, amount):
    keys = jax.random.split(key, 5)
    centre_x = jax.random.uniform(keys[0], (amount,), jnp.float32, 0.3, 0.7)
    centre_y = jax.random.uniform(keys[1], (amount,), jnp.float32, 0.3, 0.7)
    upper_dot = jax.random.randint(keys[2], (amount,), 0, 2).astype(jnp.float32)
    centre_z = 0.35 + 0.3 * upper_dot + jax.random.uniform(keys[3], (amount,), jnp.float32, -0.05, 0.05)
    spread = jax.random.uniform(keys[4], (amount,), jnp.float32, 0.12, 0.25)
    grid_x = (jnp.arange(NX, dtype=jnp.float32) + 0.5) / NX
    grid_y = (jnp.arange(NY, dtype=jnp.float32) + 0.5) / NY
    grid_z = (jnp.arange(NZ, dtype=jnp.float32) + 0.5) / NZ
    distance = (grid_x[None, :, None, None] - centre_x[:, None, None, None]) ** 2
    distance = distance + (grid_y[None, None, :, None] - centre_y[:, None, None, None]) ** 2
    distance = distance + (grid_z[None, None, None, :] - centre_z[:, None, None, None]) ** 2
    envelope = jnp.exp(-distance / (2.0 * spread[:, None, None, None] ** 2))
    return envelope.reshape(amount, NX, NY * NZ)


def draw_states(key, amount, salt):
    own_key = jax.random.fold_in(key, salt)
    keys = jax.random.split(own_key, 3)
    envelope = dot_envelopes(keys[0], amount)
    amplitude = jax.random.normal(keys[1], (amount, BANDS, 2, 1, 1), jnp.float32)
    rough = jax.random.normal(keys[2], (amount, BANDS, 2, NX, NY * NZ), jnp.float32)
    scaling = jnp.ones((amount, 1, 1, 1, 1), jnp.float32)
    modulated = (0.2 + envelope[:, None, None]) * amplitude
    spread = jnp.sqrt(modulated * modulated + 0.36)
    states = 0.25 * scaling * rough * spread
    return jnp.clip(states, -4.0, 4.0).astype(jnp.bfloat16)


def draw_electrons(key, part):
    return draw_states(key, E, 11)


def draw_holes(key, part):
    return draw_states(key, H, 12)


def setup_inputs(seed: int = 0) -> dict:
    arg_keys = jax.random.split(jax.random.key(seed), 4)
    return {
        "electrons": draw_electrons(jax.random.fold_in(arg_keys[3], 71), 0),
        "holes": draw_holes(jax.random.fold_in(arg_keys[3], 71), 0),
        "pair_order": jax.vmap(lambda own: jax.random.permutation(own, P_SIZE))(jax.random.split(arg_keys[2], GROUPS)).reshape((GROUPS, P_SIZE)).astype(jnp.int32),
    }


SCREENING = 0.01


def lattice_term(indices, points):
    return 2.0 - 2.0 * jnp.cos((2.0 * math.pi / points) * (indices % points).astype(jnp.float32))


def reference(electrons, holes, pair_order):
    index_x = jnp.arange(NX, dtype=jnp.int32)
    index_y = jnp.arange(NY, dtype=jnp.int32)
    index_z = jnp.arange(NZ, dtype=jnp.int32)
    term_x = lattice_term(index_x, NX)
    term_y = lattice_term(index_y, NY)
    term_z = lattice_term(index_z, NZ)
    green = 1.0 / (term_x[:, None, None] + term_y[None, :, None] + term_z[None, None, :] + SCREENING)
    anchor = (index_x[:, None, None] == 0) & (index_y[None, :, None] == 0) & (index_z[None, None, :] == 0)
    green = jnp.where(anchor, jnp.zeros_like(green), green)
    cells = NX * NY * NZ

    def banded(first_set, second_set):
        return jnp.einsum("ebxc,hbxc->hexc", first_set, second_set, precision=lax.Precision.HIGHEST)

    def one_group(group):
        group = group.astype(jnp.int32)
        prior = jnp.mod(group - 1 + GROUPS, GROUPS).astype(jnp.int32)
        elec = lax.dynamic_slice_in_dim(electrons, (group * EG).astype(jnp.int32), EG, 0).astype(jnp.float32)
        hole_own = lax.dynamic_slice_in_dim(holes, (group * HG).astype(jnp.int32), HG, 0)
        hole_far = lax.dynamic_slice_in_dim(holes, (prior * HG).astype(jnp.int32), HG, 0)
        hole_set = jnp.concatenate([hole_own, hole_far], axis=0).astype(jnp.float32)
        real_part = banded(elec[:, :, 0], hole_set[:, :, 0]) + banded(elec[:, :, 1], hole_set[:, :, 1])
        imag_part = banded(elec[:, :, 0], hole_set[:, :, 1]) - banded(elec[:, :, 1], hole_set[:, :, 0])
        target_shape = (P_SIZE, NX, NY, NZ)
        densities = lax.complex(real_part.reshape(target_shape), imag_part.reshape(target_shape))
        spectra = jnp.fft.fftn(densities, axes=(1, 2, 3))
        field = jnp.fft.ifftn(spectra * green[None], axes=(1, 2, 3))
        pair_rank = pair_order[group]
        field = jnp.take(field, pair_rank, axis=0)
        densities = jnp.take(densities, pair_rank, axis=0)
        flat_field = field.reshape(P_SIZE, -1)
        flat_dens = jnp.conj(densities.reshape(P_SIZE, -1))
        product = jnp.einsum("pn,qn->pq", flat_field, flat_dens, precision=lax.Precision.HIGHEST) / cells
        potential = jnp.concatenate([jnp.real(field), jnp.imag(field)], axis=-1)
        coulomb = jnp.stack([jnp.real(product), jnp.imag(product)])
        return potential, coulomb

    potential, coulomb = lax.map(one_group, jnp.arange(GROUPS, dtype=jnp.int32))
    return potential, coulomb
```

```python
import functools
import math

import jax
import jax.numpy as jnp
import numpy as np
from jax import lax
from jax.experimental import pallas as pl
from jax.experimental.pallas import tpu as pltpu
from jax.sharding import PartitionSpec as P

SCREENING = 0.01
MESH = pl.DeviceIdType.MESH
LANES = 128
F32 = jnp.float32
BF16 = jnp.bfloat16


def halves(matrix):
    high = matrix.astype(jnp.bfloat16)
    low = (matrix - high.astype(np.float64)).astype(jnp.bfloat16)
    return high, low


def phases(points):
    positions = np.arange(points)
    angles = 2.0 * math.pi / points * (np.outer(positions, positions) % points)
    return np.cos(angles), np.sin(angles)


def depth_table(points, direction):
    cosines, sines = phases(points)
    sines = direction * sines
    matrix = np.concatenate(
        [np.concatenate([cosines, -sines], 1), np.concatenate([sines, cosines], 1)], 0
    )
    high, low = halves(matrix)
    top = np.concatenate([high, low], 1)
    bottom = np.concatenate([high, np.zeros_like(high)], 1)
    return np.concatenate([top, bottom], 0)


def column_table(points, direction):
    cosines, sines = phases(points)
    high, low = halves(np.concatenate([cosines, direction * sines], 1))
    top = np.concatenate([high, high], 1)
    bottom = np.concatenate([low, np.zeros_like(low)], 1)
    return np.concatenate([top, bottom], 0)


def solver_tables(nx, ny, nz, devices):
    term_y = 2.0 - 2.0 * np.cos(2.0 * math.pi / ny * np.arange(ny))
    term_z = 2.0 - 2.0 * np.cos(2.0 * math.pi / nz * (np.arange(2 * nz) % nz))
    shift = term_y[:, None] + term_z[None, :] + SCREENING
    root = np.sqrt(shift * (shift + 4.0))
    decay = 2.0 / (shift + 2.0 + root)
    response = 1.0 / root / (ny * nz)
    anchor = np.zeros_like(shift)
    anchor[0, 0] = anchor[0, nz] = 1.0 / (SCREENING * nx * ny * nz)
    rows = nx // devices
    weights = [decay ** (rows * j) / (1.0 - decay**nx) for j in range(devices)]
    return np.stack([decay, response, anchor] + weights).astype(np.float32)


def split(values):
    high = values.astype(BF16)
    return high, (values - high.astype(F32)).astype(BF16)


def turned(values, sign):
    return pltpu.roll(values, LANES // 2, values.ndim - 1) * sign


def kernel(
    n, blocks, ny,
    order_ref, e_hbm, h_hbm, zf_ref, zi_ref, yf_ref, yi_ref, tab_ref,
    out_ref, coul_ref,
    e_ref, h_ref, prev_ref, acc_ref, rho_ref, fld_ref, res_ref, msg_ref, recv_ref,
    part_ref, peer_ref,
    load_sem, hole_send, hole_recv, msg_send, msg_recv, part_send, part_recv,
):
    bands, _, rows, cells = e_ref.shape
    tiles = cells // LANES
    group = lax.axis_index("blk")
    me = lax.axis_index("space")
    following = lax.rem(group + 1, blocks)
    preceding = lax.rem(group + blocks - 1, blocks)
    others = [lax.rem(me + j, n) for j in range(1, n)]

    loads = [
        pltpu.make_async_copy(e_hbm.at[0], e_ref, load_sem.at[0]),
        pltpu.make_async_copy(h_hbm.at[0], h_ref, load_sem.at[1]),
    ]
    for copy in loads:
        copy.start()

    barrier = pltpu.get_barrier_semaphore()
    for neighbour in (following, preceding):
        pl.semaphore_signal(barrier, inc=1, device_id=(neighbour, me), device_id_type=MESH)
    for other in others:
        pl.semaphore_signal(barrier, inc=1, device_id=(group, other), device_id_type=MESH)
    pl.semaphore_wait(barrier, n + 1)

    hole_copies = [
        pltpu.make_async_remote_copy(
            src_ref=h_hbm.at[0, b], dst_ref=prev_ref.at[b],
            send_sem=hole_send.at[b], recv_sem=hole_recv.at[b],
            device_id=(following, me), device_id_type=MESH,
        )
        for b in range(bands)
    ]
    for copy in hole_copies:
        copy.start()

    lane = lax.broadcasted_iota(jnp.int32, (1, LANES), 1)
    first_half = lane < LANES // 2
    sign = jnp.where(first_half, 1.0, -1.0).astype(F32)

    def products(holes, band_list, t, real, imag):
        window = pl.ds(pl.multiple_of(t * LANES, LANES), LANES)
        for b in band_list:
            er = e_ref[b, 0, :, window].astype(F32)
            ei = e_ref[b, 1, :, window].astype(F32)
            hr = holes[b, 0, :, window].astype(F32)
            hi = holes[b, 1, :, window].astype(F32)
            real = real + (er * hr + ei * hi)
            imag = imag + (er * hi - ei * hr)
        return real, imag

    def place(c, t, real, imag):
        moved_real = pltpu.roll(real, LANES // 2, 1)
        moved_imag = pltpu.roll(imag, LANES // 2, 1)
        rho_ref[c, pl.ds(2 * t, rows, stride=ny), :] = jnp.where(first_half, real, moved_imag)
        rho_ref[c, pl.ds(2 * t + 1, rows, stride=ny), :] = jnp.where(first_half, moved_real, imag)

    planes = min(rows, 4)
    chunk = planes * ny

    def transform(values, z_ref, y_ref):
        high, low = split(values)
        wide = jnp.dot(
            jnp.concatenate([high, low], 1), z_ref[...], preferred_element_type=F32
        )
        deep = wide[:, :LANES] + wide[:, LANES:]
        turn = turned(deep, sign)
        high, low = split(deep)
        turn_high, turn_low = split(turn)
        parts = []
        for x in range(0, planes, 2):
            columns = []
            for k in (x, x + 1):
                own = slice(k * ny, (k + 1) * ny)
                columns.append(
                    jnp.concatenate([high[own], turn_high[own], low[own], turn_low[own]], 0)
                )
            both = jnp.dot(
                y_ref[...], jnp.concatenate(columns, 1), preferred_element_type=F32
            )
            total = both[:ny] + both[ny:]
            parts += [total[:, :LANES], total[:, LANES:]]
        return jnp.concatenate(parts, 0)

    def forward(c):
        @pl.loop(0, rows // planes)
        def _(i):
            own = pl.ds(pl.multiple_of(i * chunk, chunk), chunk)
            rho_ref[c, own, :] = transform(rho_ref[c, own, :], zf_ref, yf_ref)

    block = 16

    def moments(c):
        @pl.loop(0, ny // block)
        def _(i):
            at = pl.multiple_of(i * block, block)
            decay = tab_ref[0, pl.ds(at, block), :]
            left = jnp.zeros((block, LANES), F32)
            right = jnp.zeros((block, LANES), F32)
            for x in range(rows):
                left = decay * left + rho_ref[c, pl.ds(x * ny + at, block), :]
                y = rows - 1 - x
                right = decay * right + rho_ref[c, pl.ds(y * ny + at, block), :]
            msg_ref[c, pl.ds(at, block), :] = left
            msg_ref[c, pl.ds(ny + at, block), :] = right

        total = rho_ref[c, 0:8, :]
        for x in range(1, rows):
            total = total + rho_ref[c, x * ny : x * ny + 8, :]
        msg_ref[c, 2 * ny : 2 * ny + 8, :] = total
        copies = [
            pltpu.make_async_remote_copy(
                src_ref=msg_ref.at[c], dst_ref=recv_ref.at[c, j],
                send_sem=msg_send.at[c, j], recv_sem=msg_recv.at[c, j],
                device_id=(group, others[j]), device_id_type=MESH,
            )
            for j in range(n - 1)
        ]
        for copy in copies:
            copy.start()
        return copies

    def solve(c):
        mean = msg_ref[c, 2 * ny : 2 * ny + 8, :]
        for j in range(n - 1):
            mean = mean + recv_ref[c, j, 2 * ny : 2 * ny + 8, :]
        mean = jnp.concatenate([mean, mean], 0)

        def body(i, energy):
            at = pl.multiple_of(i * block, block)
            decay = tab_ref[0, pl.ds(at, block), :]
            response = tab_ref[1, pl.ds(at, block), :]
            background = tab_ref[2, pl.ds(at, block), :] * mean
            last = tab_ref[2 + n, pl.ds(at, block), :]
            left = last * msg_ref[c, pl.ds(at, block), :]
            right = last * msg_ref[c, pl.ds(ny + at, block), :]
            for j in range(1, n):
                weight = tab_ref[2 + j, pl.ds(at, block), :]
                left = left + weight * recv_ref[c, j - 1, pl.ds(at, block), :]
                right = right + weight * recv_ref[c, n - j - 1, pl.ds(ny + at, block), :]
            spread = []
            for x in reversed(range(rows)):
                right = decay * right
                spread.append(right)
                right = right + rho_ref[c, pl.ds(x * ny + at, block), :]
            for x in range(rows):
                value = rho_ref[c, pl.ds(x * ny + at, block), :]
                left = decay * left + value
                field = response * (left + spread[rows - 1 - x]) - background
                fld_ref[c, pl.ds(x * ny + at, block), :] = field
                energy = energy + field * value
            return energy

        return lax.fori_loop(0, ny // block, body, jnp.zeros((block, LANES), F32))

    for copy in loads:
        copy.wait()

    zero = jnp.zeros((rows, LANES), F32)

    @pl.loop(0, tiles)
    def _(t):
        place(0, t, *products(h_ref, range(bands), t, zero, zero))

    forward(0)
    copies0 = moments(0)

    for b in range(bands):
        hole_copies[b].wait_recv()
        if b == 1:
            for copy in copies0:
                copy.wait_recv()
            part_ref[0:block, :] = solve(0)

            @pl.loop(0, rows // planes)
            def _(i):
                own = pl.ds(pl.multiple_of(i * chunk, chunk), chunk)
                res_ref[own, :] = transform(fld_ref[0, own, :], zi_ref, yi_ref)

        @pl.loop(0, tiles)
        def _(t, b=b):
            window = pl.ds(pl.multiple_of(t * LANES, LANES), LANES)
            if b == 0:
                real, imag = zero, zero
            else:
                real, imag = acc_ref[0, :, window], acc_ref[1, :, window]
            real, imag = products(prev_ref, [b], t, real, imag)
            if b == bands - 1:
                place(1, t, real, imag)
            else:
                acc_ref[0, :, window] = real
                acc_ref[1, :, window] = imag

    forward(1)
    copies1 = moments(1)

    def cross(i, sums):
        at = pl.ds(pl.multiple_of(i * block, block), block)
        field = fld_ref[0, at, :]
        value = rho_ref[1, at, :]
        return sums[0] + field * value, sums[1] - field * turned(value, sign)

    empty = jnp.zeros((block, LANES), F32)
    real, imag = lax.fori_loop(0, rows * ny // block, cross, (empty, empty), unroll=4)
    part_ref[2 * block : 3 * block, :] = real
    part_ref[3 * block : 4 * block, :] = imag

    for copy in copies1:
        copy.wait_recv()
    part_ref[block : 2 * block, :] = solve(1)
    part_copies = [
        pltpu.make_async_remote_copy(
            src_ref=part_ref, dst_ref=peer_ref.at[j],
            send_sem=part_send.at[j], recv_sem=part_recv.at[j],
            device_id=(group, others[j]), device_id_type=MESH,
        )
        for j in range(n - 1)
    ]
    for copy in part_copies:
        copy.start()

    order = [order_ref[0, p] for p in range(2)]

    @pl.loop(0, rows // planes)
    def _(i):
        own = pl.ds(pl.multiple_of(i * chunk, chunk), chunk)
        values = transform(fld_ref[1, own, :], zi_ref, yi_ref)
        stored = res_ref[own, :]
        for p in range(2):
            out_ref[p, own, :] = jnp.where(order[p] == 0, stored, values)

    for copy in part_copies:
        copy.wait_recv()
    entries = []
    for k in range(4):
        own = slice(k * block, (k + 1) * block)
        total = part_ref[own, :]
        for j in range(n - 1):
            total = total + peer_ref[j, own, :]
        entries.append(jnp.sum(total) * (1.0 / (n * rows * cells)))
    for p in range(2):
        for q in range(2):
            same = order[p] == order[q]
            first = order[p] == 0
            coul_ref[2 * p + q] = jnp.where(
                same, jnp.where(first, entries[0], entries[1]), entries[2]
            )
            coul_ref[4 + 2 * p + q] = jnp.where(
                same, 0.0, jnp.where(first, entries[3], -entries[3])
            )

    for copy in hole_copies + copies0 + copies1 + part_copies:
        copy.wait_send()


def shards(n, blocks, electrons, holes, pair_order):
    _, bands, parts, rows, cells = electrons.shape
    ny = nz = math.isqrt(cells)
    flat = rows * ny
    nx = rows * n
    block = 16
    vmem = pl.BlockSpec(memory_space=pltpu.VMEM)
    smem = pl.BlockSpec(memory_space=pltpu.SMEM)
    hbm = pl.BlockSpec(memory_space=pl.ANY)
    states = (bands, parts, rows, cells)
    message = 2 * ny + 8
    potential, coulomb = pl.pallas_call(
        functools.partial(kernel, n, blocks, ny),
        out_shape=(
            jax.ShapeDtypeStruct((2, flat, LANES), F32),
            jax.ShapeDtypeStruct((8,), F32),
        ),
        in_specs=[smem, hbm, hbm, vmem, vmem, vmem, vmem, vmem],
        out_specs=(vmem, smem),
        scratch_shapes=[
            pltpu.VMEM(states, BF16),
            pltpu.VMEM(states, BF16),
            pltpu.VMEM(states, BF16),
            pltpu.VMEM((2, rows, cells), F32),
            pltpu.VMEM((2, flat, LANES), F32),
            pltpu.VMEM((2, flat, LANES), F32),
            pltpu.VMEM((flat, LANES), F32),
            pltpu.VMEM((2, message, LANES), F32),
            pltpu.VMEM((2, n - 1, message, LANES), F32),
            pltpu.VMEM((4 * block, LANES), F32),
            pltpu.VMEM((n - 1, 4 * block, LANES), F32),
            pltpu.SemaphoreType.DMA((2,)),
            pltpu.SemaphoreType.DMA((bands,)),
            pltpu.SemaphoreType.DMA((bands,)),
            pltpu.SemaphoreType.DMA((2, n - 1)),
            pltpu.SemaphoreType.DMA((2, n - 1)),
            pltpu.SemaphoreType.DMA((n - 1,)),
            pltpu.SemaphoreType.DMA((n - 1,)),
        ],
        compiler_params=pltpu.CompilerParams(
            collective_id=0, has_side_effects=True, vmem_limit_bytes=40 * 1024 * 1024
        ),
        name="screened",
    )(
        pair_order,
        electrons,
        holes,
        jnp.asarray(depth_table(nz, 1.0)),
        jnp.asarray(depth_table(nz, -1.0)),
        jnp.asarray(column_table(ny, 1.0)),
        jnp.asarray(column_table(ny, -1.0)),
        jnp.asarray(solver_tables(nx, ny, nz, n)),
    )
    return potential.reshape(1, 2, rows, ny, 2 * nz), coulomb.reshape(1, 2, 2, 2)


def solution(mesh):
    body = functools.partial(shards, mesh.shape["space"], mesh.shape["blk"])
    in_specs = (
        P("blk", None, None, "space", None),
        P("blk", None, None, "space", None),
        P("blk", None),
    )
    out_specs = (P("blk", None, "space", None, None), P("blk", None, None, None))
    return jax.shard_map(body, mesh=mesh, in_specs=in_specs, out_specs=out_specs, check_vma=False)
```

```python
import functools
import math

import jax
import jax.numpy as jnp
import numpy as np
from jax import lax
from jax.experimental import pallas as pl
from jax.experimental.pallas import tpu as pltpu
from jax.sharding import PartitionSpec as P

SCREENING = 0.01
MESH = pl.DeviceIdType.MESH
LANES = 128
F32 = jnp.float32
BF16 = jnp.bfloat16


def halves(matrix):
    high = matrix.astype(jnp.bfloat16)
    low = (matrix - high.astype(np.float64)).astype(jnp.bfloat16)
    return high, low


def phases(points):
    positions = np.arange(points)
    angles = 2.0 * math.pi / points * (np.outer(positions, positions) % points)
    return np.cos(angles), np.sin(angles)


def depth_table(points, direction):
    cosines, sines = phases(points)
    sines = direction * sines
    matrix = np.concatenate(
        [np.concatenate([cosines, -sines], 1), np.concatenate([sines, cosines], 1)], 0
    )
    high, low = halves(matrix)
    top = np.concatenate([high, low], 1)
    bottom = np.concatenate([high, np.zeros_like(high)], 1)
    return np.concatenate([top, bottom], 0)


def column_table(points, direction):
    cosines, sines = phases(points)
    high, low = halves(np.concatenate([cosines, direction * sines], 1))
    top = np.concatenate([high, high], 1)
    bottom = np.concatenate([low, np.zeros_like(low)], 1)
    return np.concatenate([top, bottom], 0)


def solver_tables(nx, ny, nz, devices):
    term_y = 2.0 - 2.0 * np.cos(2.0 * math.pi / ny * np.arange(ny))
    term_z = 2.0 - 2.0 * np.cos(2.0 * math.pi / nz * (np.arange(2 * nz) % nz))
    shift = term_y[:, None] + term_z[None, :] + SCREENING
    root = np.sqrt(shift * (shift + 4.0))
    decay = 2.0 / (shift + 2.0 + root)
    response = 1.0 / root / (ny * nz)
    anchor = np.zeros_like(shift)
    anchor[0, 0] = anchor[0, nz] = 1.0 / (SCREENING * nx * ny * nz)
    rows = nx // devices
    weights = [decay ** (rows * j) / (1.0 - decay**nx) for j in range(devices)]
    return np.stack([decay, response, anchor] + weights).astype(np.float32)


def split(values):
    high = values.astype(BF16)
    return high, (values - high.astype(F32)).astype(BF16)


def turned(values, sign):
    return pltpu.roll(values, LANES // 2, values.ndim - 1) * sign


def kernel(
    n, blocks, ny,
    order_hbm, e_hbm, h_hbm, phase_hbm, tab_hbm,
    out_ref, coul_ref,
    e_ref, h_ref, prev_ref, acc_ref, rho_ref, fld_ref, res_ref, msg_ref, recv_ref,
    part_ref, peer_ref, order_ref, phase_ref, tab_ref,
    load_sem, hole_send, hole_recv, msg_send, msg_recv, part_send, part_recv,
):
    bands, _, rows, cells = e_ref.shape
    tiles = cells // LANES
    group = lax.axis_index("blk")
    me = lax.axis_index("space")
    following = lax.rem(group + 1, blocks)
    preceding = lax.rem(group + blocks - 1, blocks)
    others = [lax.rem(me + j, n) for j in range(1, n)]

    loads = [
        pltpu.make_async_copy(e_hbm.at[0], e_ref, load_sem.at[0]),
        pltpu.make_async_copy(h_hbm.at[0], h_ref, load_sem.at[1]),
        pltpu.make_async_copy(phase_hbm, phase_ref, load_sem.at[2]),
        pltpu.make_async_copy(tab_hbm, tab_ref, load_sem.at[3]),
        pltpu.make_async_copy(order_hbm, order_ref, load_sem.at[4]),
    ]
    wide = 2 * LANES
    zf_ref = phase_ref.at[0:wide]
    zi_ref = phase_ref.at[wide : 2 * wide]
    yf_ref = phase_ref.at[2 * wide : 2 * wide + LANES]
    yi_ref = phase_ref.at[2 * wide + LANES : 3 * wide]
    for copy in loads:
        copy.start()

    barrier = pltpu.get_barrier_semaphore()
    for neighbour in (following, preceding):
        pl.semaphore_signal(barrier, inc=1, device_id=(neighbour, me), device_id_type=MESH)
    for other in others:
        pl.semaphore_signal(barrier, inc=1, device_id=(group, other), device_id_type=MESH)
    pl.semaphore_wait(barrier, n + 1)

    hole_copies = [
        pltpu.make_async_remote_copy(
            src_ref=h_hbm.at[0, b], dst_ref=prev_ref.at[b],
            send_sem=hole_send.at[b], recv_sem=hole_recv.at[b],
            device_id=(following, me), device_id_type=MESH,
        )
        for b in range(bands)
    ]
    for copy in hole_copies:
        copy.start()

    lane = lax.broadcasted_iota(jnp.int32, (1, LANES), 1)
    first_half = lane < LANES // 2
    sign = jnp.where(first_half, 1.0, -1.0).astype(F32)

    def products(holes, band_list, t, real, imag):
        window = pl.ds(pl.multiple_of(t * LANES, LANES), LANES)
        for b in band_list:
            er = e_ref[b, 0, :, window].astype(F32)
            ei = e_ref[b, 1, :, window].astype(F32)
            hr = holes[b, 0, :, window].astype(F32)
            hi = holes[b, 1, :, window].astype(F32)
            real = real + (er * hr + ei * hi)
            imag = imag + (er * hi - ei * hr)
        return real, imag

    def place(c, t, real, imag):
        moved_real = pltpu.roll(real, LANES // 2, 1)
        moved_imag = pltpu.roll(imag, LANES // 2, 1)
        rho_ref[c, pl.ds(2 * t, rows, stride=ny), :] = jnp.where(first_half, real, moved_imag)
        rho_ref[c, pl.ds(2 * t + 1, rows, stride=ny), :] = jnp.where(first_half, moved_real, imag)

    planes = min(rows, 4)
    chunk = planes * ny

    def transform(values, z_ref, y_ref):
        high, low = split(values)
        wide = jnp.dot(
            jnp.concatenate([high, low], 1), z_ref[...], preferred_element_type=F32
        )
        deep = wide[:, :LANES] + wide[:, LANES:]
        turn = turned(deep, sign)
        high, low = split(deep)
        turn_high, turn_low = split(turn)
        parts = []
        for x in range(0, planes, 2):
            columns = []
            for k in (x, x + 1):
                own = slice(k * ny, (k + 1) * ny)
                columns.append(
                    jnp.concatenate([high[own], turn_high[own], low[own], turn_low[own]], 0)
                )
            both = jnp.dot(
                y_ref[...], jnp.concatenate(columns, 1), preferred_element_type=F32
            )
            total = both[:ny] + both[ny:]
            parts += [total[:, :LANES], total[:, LANES:]]
        return jnp.concatenate(parts, 0)

    def forward(c):
        @pl.loop(0, rows // planes)
        def _(i):
            own = pl.ds(pl.multiple_of(i * chunk, chunk), chunk)
            rho_ref[c, own, :] = transform(rho_ref[c, own, :], zf_ref, yf_ref)

    block = 16

    def moments(c):
        @pl.loop(0, ny // block)
        def _(i):
            at = pl.multiple_of(i * block, block)
            decay = tab_ref[0, pl.ds(at, block), :]
            left = jnp.zeros((block, LANES), F32)
            right = jnp.zeros((block, LANES), F32)
            for x in range(rows):
                left = decay * left + rho_ref[c, pl.ds(x * ny + at, block), :]
                y = rows - 1 - x
                right = decay * right + rho_ref[c, pl.ds(y * ny + at, block), :]
            msg_ref[c, pl.ds(at, block), :] = left
            msg_ref[c, pl.ds(ny + at, block), :] = right

        total = rho_ref[c, 0:8, :]
        for x in range(1, rows):
            total = total + rho_ref[c, x * ny : x * ny + 8, :]
        msg_ref[c, 2 * ny : 2 * ny + 8, :] = total
        copies = [
            pltpu.make_async_remote_copy(
                src_ref=msg_ref.at[c], dst_ref=recv_ref.at[c, j],
                send_sem=msg_send.at[c, j], recv_sem=msg_recv.at[c, j],
                device_id=(group, others[j]), device_id_type=MESH,
            )
            for j in range(n - 1)
        ]
        for copy in copies:
            copy.start()
        return copies

    def solve(c):
        mean = msg_ref[c, 2 * ny : 2 * ny + 8, :]
        for j in range(n - 1):
            mean = mean + recv_ref[c, j, 2 * ny : 2 * ny + 8, :]
        mean = jnp.concatenate([mean, mean], 0)

        def body(i, energy):
            at = pl.multiple_of(i * block, block)
            decay = tab_ref[0, pl.ds(at, block), :]
            response = tab_ref[1, pl.ds(at, block), :]
            background = tab_ref[2, pl.ds(at, block), :] * mean
            last = tab_ref[2 + n, pl.ds(at, block), :]
            left = last * msg_ref[c, pl.ds(at, block), :]
            right = last * msg_ref[c, pl.ds(ny + at, block), :]
            for j in range(1, n):
                weight = tab_ref[2 + j, pl.ds(at, block), :]
                left = left + weight * recv_ref[c, j - 1, pl.ds(at, block), :]
                right = right + weight * recv_ref[c, n - j - 1, pl.ds(ny + at, block), :]
            spread = []
            for x in reversed(range(rows)):
                right = decay * right
                spread.append(right)
                right = right + rho_ref[c, pl.ds(x * ny + at, block), :]
            for x in range(rows):
                value = rho_ref[c, pl.ds(x * ny + at, block), :]
                left = decay * left + value
                field = response * (left + spread[rows - 1 - x]) - background
                fld_ref[c, pl.ds(x * ny + at, block), :] = field
                energy = energy + field * value
            return energy

        return lax.fori_loop(0, ny // block, body, jnp.zeros((block, LANES), F32))

    for copy in loads:
        copy.wait()

    zero = jnp.zeros((rows, LANES), F32)

    @pl.loop(0, tiles)
    def _(t):
        place(0, t, *products(h_ref, range(bands), t, zero, zero))

    forward(0)
    copies0 = moments(0)

    for b in range(bands):
        hole_copies[b].wait_recv()
        if b == 1:
            for copy in copies0:
                copy.wait_recv()
            part_ref[0:block, :] = solve(0)

            @pl.loop(0, rows // planes)
            def _(i):
                own = pl.ds(pl.multiple_of(i * chunk, chunk), chunk)
                res_ref[own, :] = transform(fld_ref[0, own, :], zi_ref, yi_ref)

        @pl.loop(0, tiles)
        def _(t, b=b):
            window = pl.ds(pl.multiple_of(t * LANES, LANES), LANES)
            if b == 0:
                real, imag = zero, zero
            else:
                real, imag = acc_ref[0, :, window], acc_ref[1, :, window]
            real, imag = products(prev_ref, [b], t, real, imag)
            if b == bands - 1:
                place(1, t, real, imag)
            else:
                acc_ref[0, :, window] = real
                acc_ref[1, :, window] = imag

    forward(1)
    copies1 = moments(1)

    def cross(i, sums):
        at = pl.ds(pl.multiple_of(i * block, block), block)
        field = fld_ref[0, at, :]
        value = rho_ref[1, at, :]
        return sums[0] + field * value, sums[1] - field * turned(value, sign)

    empty = jnp.zeros((block, LANES), F32)
    real, imag = lax.fori_loop(0, rows * ny // block, cross, (empty, empty), unroll=4)
    part_ref[2 * block : 3 * block, :] = real
    part_ref[3 * block : 4 * block, :] = imag

    for copy in copies1:
        copy.wait_recv()
    part_ref[block : 2 * block, :] = solve(1)
    part_copies = [
        pltpu.make_async_remote_copy(
            src_ref=part_ref, dst_ref=peer_ref.at[j],
            send_sem=part_send.at[j], recv_sem=part_recv.at[j],
            device_id=(group, others[j]), device_id_type=MESH,
        )
        for j in range(n - 1)
    ]
    for copy in part_copies:
        copy.start()

    order = [order_ref[0, p] for p in range(2)]

    @pl.loop(0, rows // planes)
    def _(i):
        own = pl.ds(pl.multiple_of(i * chunk, chunk), chunk)
        values = transform(fld_ref[1, own, :], zi_ref, yi_ref)
        stored = res_ref[own, :]
        for p in range(2):
            out_ref[p, own, :] = jnp.where(order[p] == 0, stored, values)

    for copy in part_copies:
        copy.wait_recv()
    entries = []
    for k in range(4):
        own = slice(k * block, (k + 1) * block)
        total = part_ref[own, :]
        for j in range(n - 1):
            total = total + peer_ref[j, own, :]
        entries.append(jnp.sum(total) * (1.0 / (n * rows * cells)))
    shape = (2, 2, 2)
    part_of = lax.broadcasted_iota(jnp.int32, shape, 0)
    row = lax.broadcasted_iota(jnp.int32, shape, 1)
    column = lax.broadcasted_iota(jnp.int32, shape, 2)
    row_pair = jnp.where(row == 0, order[0], order[1])
    column_pair = jnp.where(column == 0, order[0], order[1])
    same = row_pair == column_pair
    first = row_pair == 0
    real = jnp.where(same, jnp.where(first, entries[0], entries[1]), entries[2])
    imag = jnp.where(same, 0.0, jnp.where(first, entries[3], -entries[3]))
    coul_ref[0] = jnp.where(part_of == 0, real, imag)

    for copy in hole_copies + copies0 + copies1 + part_copies:
        copy.wait_send()


def shards(n, blocks, electrons, holes, pair_order):
    _, bands, parts, rows, cells = electrons.shape
    ny = nz = math.isqrt(cells)
    flat = rows * ny
    nx = rows * n
    block = 16
    vmem = pl.BlockSpec(memory_space=pltpu.VMEM)
    hbm = pl.BlockSpec(memory_space=pl.ANY)
    states = (bands, parts, rows, cells)
    message = 2 * ny + 8
    phase = np.concatenate(
        [depth_table(nz, 1.0), depth_table(nz, -1.0), column_table(ny, 1.0), column_table(ny, -1.0)]
    )
    tables = solver_tables(nx, ny, nz, n)
    potential, coulomb = pl.pallas_call(
        functools.partial(kernel, n, blocks, ny),
        out_shape=(
            jax.ShapeDtypeStruct((2, flat, LANES), F32),
            jax.ShapeDtypeStruct((1, 2, 2, 2), F32),
        ),
        in_specs=[hbm] * 5,
        out_specs=(vmem, vmem),
        scratch_shapes=[
            pltpu.VMEM(states, BF16),
            pltpu.VMEM(states, BF16),
            pltpu.VMEM(states, BF16),
            pltpu.VMEM((2, rows, cells), F32),
            pltpu.VMEM((2, flat, LANES), F32),
            pltpu.VMEM((2, flat, LANES), F32),
            pltpu.VMEM((flat, LANES), F32),
            pltpu.VMEM((2, message, LANES), F32),
            pltpu.VMEM((2, n - 1, message, LANES), F32),
            pltpu.VMEM((4 * block, LANES), F32),
            pltpu.VMEM((n - 1, 4 * block, LANES), F32),
            pltpu.SMEM((1, 2), jnp.int32),
            pltpu.VMEM(phase.shape, BF16),
            pltpu.VMEM(tables.shape, F32),
            pltpu.SemaphoreType.DMA((5,)),
            pltpu.SemaphoreType.DMA((bands,)),
            pltpu.SemaphoreType.DMA((bands,)),
            pltpu.SemaphoreType.DMA((2, n - 1)),
            pltpu.SemaphoreType.DMA((2, n - 1)),
            pltpu.SemaphoreType.DMA((n - 1,)),
            pltpu.SemaphoreType.DMA((n - 1,)),
        ],
        compiler_params=pltpu.CompilerParams(
            collective_id=0, has_side_effects=True, vmem_limit_bytes=67_043_328
        ),
        name="screened",
    )(
        pair_order,
        electrons,
        holes,
        jnp.asarray(phase),
        jnp.asarray(tables),
    )
    return potential.reshape(1, 2, rows, ny, 2 * nz), coulomb


def solution(mesh):
    body = functools.partial(shards, mesh.shape["space"], mesh.shape["blk"])
    in_specs = (
        P("blk", None, None, "space", None),
        P("blk", None, None, "space", None),
        P("blk", None),
    )
    out_specs = (P("blk", None, "space", None, None), P("blk", None, None, None))
    return jax.shard_map(body, mesh=mesh, in_specs=in_specs, out_specs=out_specs, check_vma=False)
```

```python
import functools
import math

import jax
import jax.numpy as jnp
import numpy as np
from jax import lax
from jax.experimental import pallas as pl
from jax.experimental.pallas import tpu as pltpu
from jax.sharding import PartitionSpec as P

SCREENING = 0.01
MESH = pl.DeviceIdType.MESH
LANES = 128
F32 = jnp.float32
BF16 = jnp.bfloat16


def halves(matrix):
    high = matrix.astype(jnp.bfloat16)
    low = (matrix - high.astype(np.float64)).astype(jnp.bfloat16)
    return high, low


def phases(points):
    positions = np.arange(points)
    angles = 2.0 * math.pi / points * (np.outer(positions, positions) % points)
    return np.cos(angles), np.sin(angles)


def depth_table(points, direction):
    cosines, sines = phases(points)
    sines = direction * sines
    matrix = np.concatenate(
        [np.concatenate([cosines, -sines], 1), np.concatenate([sines, cosines], 1)], 0
    )
    high, low = halves(matrix)
    top = np.concatenate([high, low], 1)
    bottom = np.concatenate([high, np.zeros_like(high)], 1)
    return np.concatenate([top, bottom], 0)


def column_table(points, direction):
    cosines, sines = phases(points)
    high, low = halves(np.concatenate([cosines, direction * sines], 1))
    top = np.concatenate([high, high], 1)
    bottom = np.concatenate([low, np.zeros_like(low)], 1)
    return np.concatenate([top, bottom], 0)


def solver_tables(nx, ny, nz, devices):
    term_y = 2.0 - 2.0 * np.cos(2.0 * math.pi / ny * np.arange(ny))
    term_z = 2.0 - 2.0 * np.cos(2.0 * math.pi / nz * (np.arange(2 * nz) % nz))
    shift = term_y[:, None] + term_z[None, :] + SCREENING
    root = np.sqrt(shift * (shift + 4.0))
    decay = 2.0 / (shift + 2.0 + root)
    response = 1.0 / root / (ny * nz)
    anchor = np.zeros_like(shift)
    anchor[0, 0] = anchor[0, nz] = 1.0 / (SCREENING * nx * ny * nz)
    rows = nx // devices
    weights = [decay ** (rows * j) / (1.0 - decay**nx) for j in range(devices)]
    return np.stack([decay, response, anchor] + weights).astype(np.float32)


def split(values):
    high = values.astype(BF16)
    return high, (values - high.astype(F32)).astype(BF16)


def turned(values, sign):
    return pltpu.roll(values, LANES // 2, values.ndim - 1) * sign


def kernel(
    n, blocks, ny,
    order_hbm, e_hbm, h_hbm, phase_hbm, tab_hbm,
    out_ref, coul_ref,
    e_ref, h_ref, prev_ref, acc_ref, rho_ref, fld_ref, res_ref, msg_ref, recv_ref,
    part_ref, peer_ref, far_ref, order_ref, phase_ref, tab_ref,
    load_sem, hole_send, hole_recv, msg_send, msg_recv, part_send, part_recv,
):
    bands, _, rows, cells = e_ref.shape
    tiles = cells // LANES
    group = lax.axis_index("blk")
    me = lax.axis_index("space")
    following = lax.rem(group + 1, blocks)
    preceding = lax.rem(group + blocks - 1, blocks)
    others = [lax.rem(me + j, n) for j in range(1, n)]

    loads = [
        pltpu.make_async_copy(e_hbm.at[0], e_ref, load_sem.at[0]),
        pltpu.make_async_copy(h_hbm.at[0], h_ref, load_sem.at[1]),
        pltpu.make_async_copy(phase_hbm, phase_ref, load_sem.at[2]),
        pltpu.make_async_copy(tab_hbm, tab_ref, load_sem.at[3]),
        pltpu.make_async_copy(order_hbm, order_ref, load_sem.at[4]),
    ]
    wide = 2 * LANES
    zf_ref = phase_ref.at[0:wide]
    zi_ref = phase_ref.at[wide : 2 * wide]
    yf_ref = phase_ref.at[2 * wide : 2 * wide + LANES]
    yi_ref = phase_ref.at[2 * wide + LANES : 3 * wide]
    for copy in loads:
        copy.start()

    barrier = pltpu.get_barrier_semaphore()
    for neighbour in (following, preceding):
        pl.semaphore_signal(barrier, inc=1, device_id=(neighbour, me), device_id_type=MESH)
    for other in others:
        pl.semaphore_signal(barrier, inc=1, device_id=(group, other), device_id_type=MESH)
    pl.semaphore_wait(barrier, n + 1)

    hole_copies = [
        pltpu.make_async_remote_copy(
            src_ref=h_hbm.at[0, b], dst_ref=prev_ref.at[b],
            send_sem=hole_send.at[b], recv_sem=hole_recv.at[b],
            device_id=(following, me), device_id_type=MESH,
        )
        for b in range(bands)
    ]
    for copy in hole_copies:
        copy.start()

    lane = lax.broadcasted_iota(jnp.int32, (1, LANES), 1)
    first_half = lane < LANES // 2
    sign = jnp.where(first_half, 1.0, -1.0).astype(F32)

    def products(holes, band_list, t, real, imag):
        window = pl.ds(pl.multiple_of(t * LANES, LANES), LANES)
        for b in band_list:
            er = e_ref[b, 0, :, window].astype(F32)
            ei = e_ref[b, 1, :, window].astype(F32)
            hr = holes[b, 0, :, window].astype(F32)
            hi = holes[b, 1, :, window].astype(F32)
            real = real + (er * hr + ei * hi)
            imag = imag + (er * hi - ei * hr)
        return real, imag

    def place(c, t, real, imag):
        moved_real = pltpu.roll(real, LANES // 2, 1)
        moved_imag = pltpu.roll(imag, LANES // 2, 1)
        rho_ref[c, pl.ds(2 * t, rows, stride=ny), :] = jnp.where(first_half, real, moved_imag)
        rho_ref[c, pl.ds(2 * t + 1, rows, stride=ny), :] = jnp.where(first_half, moved_real, imag)

    planes = min(rows, 4)
    chunk = planes * ny

    def transform(values, z_ref, y_ref):
        high, low = split(values)
        wide = jnp.dot(
            jnp.concatenate([high, low], 1), z_ref[...], preferred_element_type=F32
        )
        deep = wide[:, :LANES] + wide[:, LANES:]
        turn = turned(deep, sign)
        high, low = split(deep)
        turn_high, turn_low = split(turn)
        parts = []
        for x in range(0, planes, 2):
            columns = []
            for k in (x, x + 1):
                own = slice(k * ny, (k + 1) * ny)
                columns.append(
                    jnp.concatenate([high[own], turn_high[own], low[own], turn_low[own]], 0)
                )
            both = jnp.dot(
                y_ref[...], jnp.concatenate(columns, 1), preferred_element_type=F32
            )
            total = both[:ny] + both[ny:]
            parts += [total[:, :LANES], total[:, LANES:]]
        return jnp.concatenate(parts, 0)

    def forward(c):
        @pl.loop(0, rows // planes, unroll=min(2, rows // planes))
        def _(i):
            own = pl.ds(pl.multiple_of(i * chunk, chunk), chunk)
            rho_ref[c, own, :] = transform(rho_ref[c, own, :], zf_ref, yf_ref)

    block = 16

    def moments(c):
        @pl.loop(0, ny // block)
        def _(i):
            at = pl.multiple_of(i * block, block)
            decay = tab_ref[0, pl.ds(at, block), :]
            left = jnp.zeros((block, LANES), F32)
            right = jnp.zeros((block, LANES), F32)
            for x in range(rows):
                left = decay * left + rho_ref[c, pl.ds(x * ny + at, block), :]
                y = rows - 1 - x
                right = decay * right + rho_ref[c, pl.ds(y * ny + at, block), :]
            msg_ref[c, pl.ds(at, block), :] = left
            msg_ref[c, pl.ds(ny + at, block), :] = right

        total = rho_ref[c, 0:8, :]
        for x in range(1, rows):
            total = total + rho_ref[c, x * ny : x * ny + 8, :]
        msg_ref[c, 2 * ny : 2 * ny + 8, :] = total
        copies = [
            pltpu.make_async_remote_copy(
                src_ref=msg_ref.at[c], dst_ref=recv_ref.at[c, j],
                send_sem=msg_send.at[c, j], recv_sem=msg_recv.at[c, j],
                device_id=(group, others[j]), device_id_type=MESH,
            )
            for j in range(n - 1)
        ]
        for copy in copies:
            copy.start()
        return copies

    empty = jnp.zeros((block, LANES), F32)

    def local(c):
        def body(i, energy):
            at = pl.multiple_of(i * block, block)
            decay = tab_ref[0, pl.ds(at, block), :]
            response = tab_ref[1, pl.ds(at, block), :]
            left = right = empty
            spread = []
            for x in reversed(range(rows)):
                right = decay * right
                spread.append(right)
                right = right + rho_ref[c, pl.ds(x * ny + at, block), :]
            for x in range(rows):
                value = rho_ref[c, pl.ds(x * ny + at, block), :]
                left = decay * left + value
                field = response * (left + spread[rows - 1 - x])
                fld_ref[c, pl.ds(x * ny + at, block), :] = field
                energy = energy + field * value
            return energy

        return lax.fori_loop(0, ny // block, body, empty)

    def solve(c):
        mean = msg_ref[c, 2 * ny : 2 * ny + 8, :]
        for k in range(n - 1):
            mean = mean + recv_ref[c, k, 2 * ny : 2 * ny + 8, :]
        mean = jnp.concatenate([mean, mean], 0)

        def body(i, energy):
            at = pl.multiple_of(i * block, block)
            decay = tab_ref[0, pl.ds(at, block), :]
            response = tab_ref[1, pl.ds(at, block), :]
            background = tab_ref[2, pl.ds(at, block), :] * mean
            weights = [tab_ref[3 + k, pl.ds(at, block), :] for k in range(n)]
            rights = [msg_ref[c, pl.ds(at, block), :]]
            lefts = [msg_ref[c, pl.ds(ny + at, block), :]]
            for k in range(n - 1):
                rights.append(recv_ref[c, k, pl.ds(at, block), :])
                lefts.append(recv_ref[c, k, pl.ds(ny + at, block), :])
            left = right = pairs = empty
            for a in range(n):
                coming = empty
                for k in range(n):
                    coming = coming + weights[k] * rights[(a + k + 1) % n]
                pairs = pairs + coming * lefts[a]
                if a == 0:
                    left = coming
            for k in range(n):
                right = right + weights[k] * lefts[(n - k - 1) % n]
            energy = energy + 2.0 * response * decay * pairs - background * mean
            left = response * left
            right = response * right
            spread = []
            for x in range(rows):
                right = decay * right
                spread.append(right)
            for x in range(rows):
                left = decay * left
                own = pl.ds(x * ny + at, block)
                fld_ref[c, own, :] = fld_ref[c, own, :] + (
                    left + spread[rows - 1 - x] - background
                )
            return energy

        return lax.fori_loop(0, ny // block, body, empty)

    for copy in loads:
        copy.wait()

    zero = jnp.zeros((rows, LANES), F32)

    @pl.loop(0, tiles, unroll=4)
    def _(t):
        place(0, t, *products(h_ref, range(bands), t, zero, zero))

    forward(0)
    copies0 = moments(0)
    part_ref[0:block, :] = local(0)

    for b in range(bands):
        hole_copies[b].wait_recv()
        if b == 1:
            for copy in copies0:
                copy.wait_recv()
            far_ref[0:block, :] = solve(0)

            @pl.loop(0, rows // planes, unroll=min(2, rows // planes))
            def _(i):
                own = pl.ds(pl.multiple_of(i * chunk, chunk), chunk)
                res_ref[own, :] = transform(fld_ref[0, own, :], zi_ref, yi_ref)

        @pl.loop(0, tiles, unroll=4)
        def _(t, b=b):
            window = pl.ds(pl.multiple_of(t * LANES, LANES), LANES)
            if b == 0:
                real, imag = zero, zero
            else:
                real, imag = acc_ref[0, :, window], acc_ref[1, :, window]
            real, imag = products(prev_ref, [b], t, real, imag)
            if b == bands - 1:
                place(1, t, real, imag)
            else:
                acc_ref[0, :, window] = real
                acc_ref[1, :, window] = imag

    forward(1)
    copies1 = moments(1)
    part_ref[block : 2 * block, :] = local(1)

    def cross(i, sums):
        at = pl.ds(pl.multiple_of(i * block, block), block)
        field = fld_ref[0, at, :]
        value = rho_ref[1, at, :]
        return sums[0] + field * value, sums[1] - field * turned(value, sign)

    real, imag = lax.fori_loop(0, rows * ny // block, cross, (empty, empty), unroll=4)
    part_ref[2 * block : 3 * block, :] = real
    part_ref[3 * block : 4 * block, :] = imag
    part_copies = [
        pltpu.make_async_remote_copy(
            src_ref=part_ref, dst_ref=peer_ref.at[j],
            send_sem=part_send.at[j], recv_sem=part_recv.at[j],
            device_id=(group, others[j]), device_id_type=MESH,
        )
        for j in range(n - 1)
    ]
    for copy in part_copies:
        copy.start()

    for copy in copies1:
        copy.wait_recv()
    far_ref[block : 2 * block, :] = solve(1)

    order = [order_ref[0, p] for p in range(2)]

    @pl.loop(0, rows // planes, unroll=min(2, rows // planes))
    def _(i):
        own = pl.ds(pl.multiple_of(i * chunk, chunk), chunk)
        values = transform(fld_ref[1, own, :], zi_ref, yi_ref)
        stored = res_ref[own, :]
        for p in range(2):
            out_ref[p, own, :] = jnp.where(order[p] == 0, stored, values)

    for copy in part_copies:
        copy.wait_recv()
    entries = []
    for k in range(4):
        own = slice(k * block, (k + 1) * block)
        total = part_ref[own, :]
        for j in range(n - 1):
            total = total + peer_ref[j, own, :]
        if k < 2:
            total = total + far_ref[own, :]
        entries.append(jnp.sum(total) * (1.0 / (n * rows * cells)))
    shape = (2, 2, 2)
    part_of = lax.broadcasted_iota(jnp.int32, shape, 0)
    row = lax.broadcasted_iota(jnp.int32, shape, 1)
    column = lax.broadcasted_iota(jnp.int32, shape, 2)
    row_pair = jnp.where(row == 0, order[0], order[1])
    column_pair = jnp.where(column == 0, order[0], order[1])
    same = row_pair == column_pair
    first = row_pair == 0
    real = jnp.where(same, jnp.where(first, entries[0], entries[1]), entries[2])
    imag = jnp.where(same, 0.0, jnp.where(first, entries[3], -entries[3]))
    coul_ref[0] = jnp.where(part_of == 0, real, imag)

    for copy in hole_copies + copies0 + copies1 + part_copies:
        copy.wait_send()


def shards(n, blocks, electrons, holes, pair_order):
    _, bands, parts, rows, cells = electrons.shape
    ny = nz = math.isqrt(cells)
    flat = rows * ny
    nx = rows * n
    block = 16
    vmem = pl.BlockSpec(memory_space=pltpu.VMEM)
    hbm = pl.BlockSpec(memory_space=pl.ANY)
    states = (bands, parts, rows, cells)
    message = 2 * ny + 8
    phase = np.concatenate(
        [depth_table(nz, 1.0), depth_table(nz, -1.0), column_table(ny, 1.0), column_table(ny, -1.0)]
    )
    tables = solver_tables(nx, ny, nz, n)
    potential, coulomb = pl.pallas_call(
        functools.partial(kernel, n, blocks, ny),
        out_shape=(
            jax.ShapeDtypeStruct((2, flat, LANES), F32),
            jax.ShapeDtypeStruct((1, 2, 2, 2), F32),
        ),
        in_specs=[hbm] * 5,
        out_specs=(vmem, vmem),
        scratch_shapes=[
            pltpu.VMEM(states, BF16),
            pltpu.VMEM(states, BF16),
            pltpu.VMEM(states, BF16),
            pltpu.VMEM((2, rows, cells), F32),
            pltpu.VMEM((2, flat, LANES), F32),
            pltpu.VMEM((2, flat, LANES), F32),
            pltpu.VMEM((flat, LANES), F32),
            pltpu.VMEM((2, message, LANES), F32),
            pltpu.VMEM((2, n - 1, message, LANES), F32),
            pltpu.VMEM((4 * block, LANES), F32),
            pltpu.VMEM((n - 1, 4 * block, LANES), F32),
            pltpu.VMEM((2 * block, LANES), F32),
            pltpu.SMEM((1, 2), jnp.int32),
            pltpu.VMEM(phase.shape, BF16),
            pltpu.VMEM(tables.shape, F32),
            pltpu.SemaphoreType.DMA((5,)),
            pltpu.SemaphoreType.DMA((bands,)),
            pltpu.SemaphoreType.DMA((bands,)),
            pltpu.SemaphoreType.DMA((2, n - 1)),
            pltpu.SemaphoreType.DMA((2, n - 1)),
            pltpu.SemaphoreType.DMA((n - 1,)),
            pltpu.SemaphoreType.DMA((n - 1,)),
        ],
        compiler_params=pltpu.CompilerParams(
            collective_id=0, has_side_effects=True, vmem_limit_bytes=67_043_328
        ),
        name="screened",
    )(
        pair_order,
        electrons,
        holes,
        jnp.asarray(phase),
        jnp.asarray(tables),
    )
    return potential.reshape(1, 2, rows, ny, 2 * nz), coulomb


def solution(mesh):
    body = functools.partial(shards, mesh.shape["space"], mesh.shape["blk"])
    in_specs = (
        P("blk", None, None, "space", None),
        P("blk", None, None, "space", None),
        P("blk", None),
    )
    out_specs = (P("blk", None, "space", None, None), P("blk", None, None, None))
    return jax.shard_map(body, mesh=mesh, in_specs=in_specs, out_specs=out_specs, check_vma=False)
```
